128 devices in a mesh: req: 64 (over z, y, x_hi, core), tensor: 2 (over x_lo).
Axes of the slice: x: 4 (x_hi: 2, x_lo: 2; x = x_hi * 2 + x_lo), y: 4, z: 4, core: 2. Of those that a mesh axis runs over, the one named last changes fastest.
Arguments:
- tokens: bfloat16 [32768, 1024], P(('req', 'tensor')), may hold values from -6 to 6
- self_project: bfloat16 [3, 1024, 1024], P(None, None, 'tensor'), may hold values from -0.1875 to 0.1875
- self_output: bfloat16 [1024, 1024], P('tensor'), may hold values from -0.1875 to 0.1875
- cross_query: bfloat16 [1024, 1024], P(None, 'tensor'), may hold values from -0.1875 to 0.1875
- cross_output: bfloat16 [1024, 1024], P('tensor'), may hold values from -0.1875 to 0.1875
- expand_weight: bfloat16 [1024, 4096], P(None, 'tensor'), may hold values from -0.1875 to 0.1875
- reduce_weight: bfloat16 [4096, 1024], P('tensor'), may hold values from -0.09375 to 0.09375
- norm_gains: float32 [3, 1024], replicated, may hold values from 0.5 to 1.5
- cache_pairs: bfloat16 [131072, 2, 1024], P('req', None, 'tensor'), may hold values from -64 to 64
- encoder_pairs: bfloat16 [32768, 2, 1024], P('req', None, 'tensor'), may hold values from -64 to 64
- request_order: int32 [64], replicated, may hold values from 0 to 63, each once
- page_table: int32 [64, 32], replicated, may hold values from 0 to 2047, as said below
- cached_length: int32 [64], replicated, may hold values from 1 to 2048
- span_length: int32 [64], replicated, may hold values from 128 to 512
Outputs:
- mixed: bfloat16 [32768, 1024], P(('req', 'tensor'))
- page_pool: bfloat16 [131072, 2, 1024], P('req', None, 'tensor')
The draws below stay inside these ranges and needn't reach their ends.
Inputs may be any that keep to these rules, and one draw needn't show every extreme that they name: page_table maps all pairs of request and page one to one onto 0 .. 2047; the 32 pages of one request lie in 32 different blocks of 32 consecutive pool pages, and every such block holds one page of each page number j.
All inputs are finite; a program needn't handle non-finite values.
Results may differ from the reference program's by a relative error of at most 0.007.
The reference program's roundings to bfloat16 on the way count: a program that leaves them out, or rounds other values in their place, can miss the bound.
Values may be sent and summed in bfloat16 or wider, within the bound.
No kernel may reach another device: no remote copies, remote signals or barrier semaphores. Data moves between devices by JAX's collectives and lax.ppermute only.
A program may use at most 192 MiB of HBM per device.

```python
import jax
import jax.numpy as jnp
from jax import lax

D = 1024
HEAD = 64
FF = 4096
SPAN = 512
ENC = 512
PAGE = 64
REQUESTS = 64
PAGES_REQ = 32
CACHE = 2048
POOL = 2048


def scaled_pairs(key, total_rows):
    base = jnp.clip(jax.random.normal(jax.random.fold_in(key, 11), (total_rows, 2, D), jnp.float32), -6.0, 6.0)
    return base


def draw_cache_pairs(key, part):
    return scaled_pairs(key, REQUESTS * CACHE).astype(jnp.bfloat16)


def draw_encoder_pairs(key, part):
    return scaled_pairs(key, REQUESTS * ENC).astype(jnp.bfloat16)


def draw_page_table(key, part):
    offsets = jax.random.permutation(jax.random.fold_in(key, 21), REQUESTS)[:PAGES_REQ]
    shuffle = jax.random.permutation(jax.random.fold_in(key, 22), REQUESTS)
    relabel = jax.random.permutation(jax.random.fold_in(key, 23), REQUESTS)
    target_block = relabel[(shuffle[:, None] + offsets[None, :]) % REQUESTS]
    scores = jax.random.randint(jax.random.fold_in(key, 24), (REQUESTS, PAGES_REQ), 0, 1 << 20) * PAGES_REQ + jnp.arange(PAGES_REQ, dtype=jnp.int32)[None, :]
    placing = jnp.argsort(scores, axis=1, stable=True).astype(jnp.int32)
    within = placing[target_block, jnp.arange(PAGES_REQ, dtype=jnp.int32)[None, :]]
    return (target_block * PAGES_REQ + within).astype(jnp.int32)


def draw_cached_length(key, part):
    values = jax.random.randint(jax.random.fold_in(key, 31), (REQUESTS,), 1, CACHE + 1)
    chosen = jax.random.randint(jax.random.fold_in(key, 32), (), 0, REQUESTS)
    return jnp.where(jnp.arange(REQUESTS, dtype=jnp.int32) == chosen, CACHE, values).astype(jnp.int32)


def draw_span_length(key, part):
    values = jax.random.randint(jax.random.fold_in(key, 41), (REQUESTS,), SPAN // 4, SPAN + 1)
    chosen = jax.random.randint(jax.random.fold_in(key, 42), (), 0, REQUESTS)
    return jnp.where(jnp.arange(REQUESTS, dtype=jnp.int32) == chosen, SPAN, values).astype(jnp.int32)


def level_of(own_key, dims, split, smallest, largest):
    level = 1.0
    for dim, blocks in split:
        heights = jax.random.uniform(jax.random.fold_in(jax.random.fold_in(own_key, 6), dim), (blocks,), jnp.float32, smallest / len(split), largest / len(split))
        level = level * jnp.repeat(jnp.exp(heights), dims[dim] // blocks).reshape((-1,) + (1,) * (len(dims) - 1 - dim))
    return level


def normal_values(stream_key, dims, scale, bound, pieces=(), held_as=jnp.bfloat16):
    result = scale * jax.random.normal(stream_key, dims, jnp.float32)
    if pieces:
        result = result * level_of(stream_key, dims, pieces, -0.22, 0.18)
    return jnp.clip(result, -bound, bound).astype(held_as)


def setup_inputs(seed: int = 0) -> dict:
    key_list = jax.random.split(jax.random.key(seed), 15)
    tokens = normal_values(key_list[0], (REQUESTS * SPAN, D), 1.0, 6.0, ((0, 128),))
    self_project = normal_values(key_list[1], (3, D, D), D ** -0.5, 0.1875, ((2, 2),))
    self_output = normal_values(key_list[2], (D, D), D ** -0.5, 0.1875, ((0, 2),))
    cross_query = normal_values(key_list[3], (D, D), D ** -0.5, 0.1875, ((1, 2),))
    cross_output = normal_values(key_list[4], (D, D), D ** -0.5, 0.1875, ((0, 2),))
    expand_weight = normal_values(key_list[5], (D, FF), D ** -0.5, 0.1875, ((1, 2),))
    reduce_weight = normal_values(key_list[6], (FF, D), FF ** -0.5, 0.09375, ((0, 2),))
    norm_gains = jnp.clip(1.0 + 0.1 * jax.random.normal(key_list[7], (3, D), jnp.float32), 0.5, 1.5)
    cache_pairs = draw_cache_pairs(jax.random.fold_in(key_list[14], 71), 0)
    encoder_pairs = draw_encoder_pairs(jax.random.fold_in(key_list[14], 71), 0)
    request_order = jax.random.permutation(key_list[10], REQUESTS).astype(jnp.int32)
    page_table = draw_page_table(jax.random.fold_in(key_list[14], 71), 0)
    cached_length = draw_cached_length(jax.random.fold_in(key_list[14], 71), 0)
    span_length = draw_span_length(jax.random.fold_in(key_list[14], 71), 0)
    return {"tokens": tokens, "self_project": self_project, "self_output": self_output, "cross_query": cross_query, "cross_output": cross_output, "expand_weight": expand_weight, "reduce_weight": reduce_weight, "norm_gains": norm_gains, "cache_pairs": cache_pairs, "encoder_pairs": encoder_pairs, "request_order": request_order, "page_table": page_table, "cached_length": cached_length, "span_length": span_length}


norm_eps = 1e-05
masked_score = -1e+30

def layer_norm(values, gain):
    center = values - lax.optimization_barrier(jnp.mean(values, axis=-1, keepdims=True))
    spread = lax.optimization_barrier(jnp.mean(center * center, axis=-1, keepdims=True))
    return center * lax.rsqrt(spread + norm_eps) * gain

def attend(queries, keys_in, values_in, allowed):
    length = queries.shape[0]
    heads_here = queries.shape[1] // HEAD
    query_heads = queries.astype(jnp.float32).reshape(length, heads_here, HEAD)
    key_heads = keys_in.astype(jnp.float32).reshape(keys_in.shape[0], heads_here, HEAD)
    value_heads = values_in.astype(jnp.float32).reshape(values_in.shape[0], heads_here, HEAD)
    scores = jnp.einsum('qhd,khd->hqk', query_heads, key_heads)
    if allowed is not None:
        scores = jnp.where(allowed[None], scores, masked_score)
    highest = lax.optimization_barrier(jnp.max(scores, axis=-1, keepdims=True))
    raised = jnp.exp(scores - highest)
    weights = (raised / lax.optimization_barrier(jnp.sum(raised, axis=-1, keepdims=True))).astype(jnp.bfloat16)
    context = jnp.einsum('hqk,khd->qhd', weights.astype(jnp.float32), value_heads)
    return context.reshape(length, heads_here * HEAD).astype(jnp.bfloat16)

def reference(tokens, self_project, self_output, cross_query, cross_output, expand_weight, reduce_weight, norm_gains, cache_pairs, encoder_pairs, request_order, page_table, cached_length, span_length):
    scaling = HEAD ** (-0.5)

    def one_request(position):
        request = request_order[position]
        live_cache = cached_length[request]
        live_span = span_length[request]
        inputs = lax.dynamic_slice_in_dim(tokens, position * SPAN, SPAN, 0)
        cached = lax.dynamic_slice_in_dim(cache_pairs, position * CACHE, CACHE, 0)
        encoded = lax.dynamic_slice_in_dim(encoder_pairs, position * ENC, ENC, 0)
        queries = (jnp.dot(inputs, self_project[0], preferred_element_type=jnp.float32) * scaling).astype(jnp.bfloat16)
        new_keys = jnp.dot(inputs, self_project[1], preferred_element_type=jnp.float32).astype(jnp.bfloat16)
        new_values = jnp.dot(inputs, self_project[2], preferred_element_type=jnp.float32).astype(jnp.bfloat16)
        keys_all = jnp.concatenate([cached[:, 0], new_keys], axis=0)
        values_all = jnp.concatenate([cached[:, 1], new_values], axis=0)
        query_index = jnp.arange(SPAN, dtype=jnp.int32)[:, None]
        cache_index = jnp.arange(CACHE, dtype=jnp.int32)[None, :]
        span_index = jnp.arange(SPAN, dtype=jnp.int32)[None, :]
        allowed = jnp.concatenate([jnp.broadcast_to(cache_index < live_cache, (SPAN, CACHE)), (span_index <= query_index) & (span_index < live_span)], axis=1)
        context = attend(queries, keys_all, values_all, allowed)
        first = layer_norm(inputs.astype(jnp.float32) + jnp.dot(context, self_output, preferred_element_type=jnp.float32), norm_gains[0]).astype(jnp.bfloat16)
        cross_queries = (jnp.dot(first, cross_query, preferred_element_type=jnp.float32) * scaling).astype(jnp.bfloat16)
        cross_context = attend(cross_queries, encoded[:, 0], encoded[:, 1], None)
        second = layer_norm(first.astype(jnp.float32) + jnp.dot(cross_context, cross_output, preferred_element_type=jnp.float32), norm_gains[1]).astype(jnp.bfloat16)
        expanded = jax.nn.gelu(jnp.dot(second, expand_weight, preferred_element_type=jnp.float32), approximate=False).astype(jnp.bfloat16)
        final = layer_norm(second.astype(jnp.float32) + jnp.dot(expanded, reduce_weight, preferred_element_type=jnp.float32), norm_gains[2])
        final = jnp.where(query_index < live_span, final, 0.0)
        return final.astype(jnp.bfloat16)
    blocks = lax.map(one_request, jnp.arange(REQUESTS, dtype=jnp.int32))
    mixed = blocks.reshape(REQUESTS * SPAN, D)
    targets = page_table[request_order].reshape(-1)
    pages_all = cache_pairs.reshape(REQUESTS * PAGES_REQ, PAGE, 2, D)
    page_pool = jnp.zeros((POOL, PAGE, 2, D), cache_pairs.dtype).at[targets].set(pages_all)
    return (mixed, page_pool.reshape(POOL * PAGE, 2, D))
```

```python
import functools

import jax
import jax.numpy as jnp
from jax import lax
from jax.experimental import pallas as pl
from jax.experimental.pallas import tpu as pltpu
from jax.sharding import PartitionSpec as P

HEAD = 64
PAGE = 64
LANES = 128
norm_eps = 1e-05
masked_score = -1e30
VMEM_LIMIT = 60 * 1024 * 1024


ANY = pl.BlockSpec(memory_space=pl.ANY)
SMEM = pl.BlockSpec(memory_space=pltpu.SMEM)
VMEM = pl.BlockSpec(memory_space=pltpu.VMEM)


def layer_norm(values, gain):
    center = values - jnp.mean(values, axis=-1, keepdims=True)
    spread = jnp.mean(center * center, axis=-1, keepdims=True)
    return center * lax.rsqrt(spread + norm_eps) * gain


def dot(a, b):
    return jnp.dot(a, b, preferred_element_type=jnp.float32)


def dot_t(a, b):
    return lax.dot_general(a, b, (((1,), (1,)), ((), ())), preferred_element_type=jnp.float32)


def move_pages(index_ref, source, target, held, in_sem, out_sem, *, scatter):
    count = held.shape[0]

    def load(j):
        return pltpu.make_async_copy(source.at[j if scatter else index_ref[j]], held.at[j], in_sem.at[j])

    def store(j):
        return pltpu.make_async_copy(held.at[j], target.at[index_ref[j] if scatter else j], out_sem.at[j])

    for j in range(count):
        load(j).start()
    for j in range(count):
        load(j).wait()
        store(j).start()
    for j in range(count):
        store(j).wait()


def pages_call(index, source, slots, count, scatter):
    rows = source.shape[1]
    return pl.pallas_call(
        functools.partial(move_pages, scatter=scatter),
        out_shape=jax.ShapeDtypeStruct((slots, rows, LANES), jnp.bfloat16),
        in_specs=[SMEM, ANY],
        out_specs=ANY,
        scratch_shapes=[
            pltpu.VMEM((count, rows, LANES), jnp.bfloat16),
            pltpu.SemaphoreType.DMA((count,)),
            pltpu.SemaphoreType.DMA((count,)),
        ],
        compiler_params=pltpu.CompilerParams(vmem_limit_bytes=VMEM_LIMIT),
        cost_estimate=pl.CostEstimate(flops=0, bytes_accessed=4 * count * rows * LANES, transcendentals=0),
        name="pack_pages" if scatter else "unpack_pages",
    )(index, source)


def split_kernel(pairs_ref, keys_ref, values_ref):
    groups = keys_ref.shape[1] // LANES * 2
    per = 256 // groups
    row = lax.broadcasted_iota(jnp.int32, (256, 256), 0)
    col = lax.broadcasted_iota(jnp.int32, (256, 256), 1)
    pick = (col == lax.rem(row, per) * groups + lax.div(row, per)).astype(jnp.bfloat16)
    for block in range(keys_ref.shape[0] // per):
        got = dot(pick, pairs_ref[block * 256 : (block + 1) * 256, :]).astype(jnp.bfloat16)
        for tile in range(groups // 2):
            where = (pl.ds(block * per, per), pl.ds(tile * LANES, LANES))
            keys_ref[where] = got[2 * tile * per : (2 * tile + 1) * per]
            values_ref[where] = got[(2 * tile + 1) * per : (2 * tile + 2) * per]


def split_pairs(pairs, width):
    rows = pairs.shape[0] * LANES // (2 * width)
    step = 256
    out = jax.ShapeDtypeStruct((rows, width), jnp.bfloat16)
    return pl.pallas_call(
        split_kernel,
        out_shape=(out, out),
        grid=(rows // step,),
        in_specs=[pl.BlockSpec((step * 2 * width // LANES, LANES), lambda i: (i, 0))],
        out_specs=[pl.BlockSpec((step, width), lambda i: (i, 0))] * 2,
        compiler_params=pltpu.CompilerParams(vmem_limit_bytes=VMEM_LIMIT),
        cost_estimate=pl.CostEstimate(
            flops=rows * 2 * width * 512, bytes_accessed=8 * rows * width, transcendentals=0
        ),
        name="split_pairs",
    )(pairs)


def flat_pairs(pairs):
    rows, _, width = pairs.shape
    return pairs.reshape(rows, 2, width // LANES, LANES).transpose(0, 2, 1, 3).reshape(-1, LANES)


def unflat_pairs(flat, rows, width):
    return flat.reshape(rows, width // LANES, 2, LANES).transpose(0, 2, 1, 3).reshape(rows, 2, width)


def self_kernel(
    scalars, queries_ref, cached_keys, cached_values, keys_a, values_a, keys_b, values_b, out_ref
):
    live_cache, live_span, row_off, a_off, b_off = [scalars[n] for n in range(5)]
    length = queries_ref.shape[0]
    new = keys_a.shape[0]
    slot = lax.broadcasted_iota(jnp.int32, (1, cached_keys.shape[0]), 1)
    cache_live = slot < live_cache
    row = row_off + lax.broadcasted_iota(jnp.int32, (length, new), 0)
    column = lax.broadcasted_iota(jnp.int32, (length, new), 1)
    seen = [((column + off) <= row) & ((column + off) < live_span) for off in (a_off, b_off)]
    lane = lax.broadcasted_iota(jnp.int32, (length, LANES), 1)
    queries = queries_ref[...]
    contexts = []
    for half in range(LANES // HEAD):
        mine = (lane >= half * HEAD) & (lane < (half + 1) * HEAD)
        own = jnp.where(mine, queries, jnp.zeros_like(queries))
        parts = [
            jnp.where(cache_live, dot_t(own, cached_keys[...]), masked_score),
            jnp.where(seen[0], dot_t(own, keys_a[...]), masked_score),
            jnp.where(seen[1], dot_t(own, keys_b[...]), masked_score),
        ]
        highest = functools.reduce(
            jnp.maximum, [jnp.max(part, axis=-1, keepdims=True) for part in parts]
        )
        raised = [jnp.exp(part - highest) for part in parts]
        total = sum(jnp.sum(part, axis=-1, keepdims=True) for part in raised)
        scale = 1.0 / total
        context = jnp.zeros((length, LANES), jnp.float32)
        for part, values in zip(raised, (cached_values, values_a, values_b)):
            context += dot((part * scale).astype(jnp.bfloat16), values[...])
        contexts.append(context)
    out_ref[...] = jnp.where(lane < HEAD, contexts[0], contexts[1]).astype(jnp.bfloat16)


def self_attention(scalars, queries, cached, new_a, new_b):
    length, width = queries.shape
    cache_rows = cached[0].shape[0]
    new = new_a[0].shape[0]

    def spec(rows):
        return pl.BlockSpec((rows, LANES), lambda c: (0, c))

    total = cache_rows + 2 * new
    return pl.pallas_call(
        self_kernel,
        out_shape=jax.ShapeDtypeStruct((length, width), jnp.bfloat16),
        grid=(width // LANES,),
        in_specs=[SMEM, spec(length), spec(cache_rows), spec(cache_rows)] + [spec(new)] * 4,
        out_specs=spec(length),
        compiler_params=pltpu.CompilerParams(vmem_limit_bytes=VMEM_LIMIT),
        cost_estimate=pl.CostEstimate(
            flops=4 * length * total * width * 4,
            bytes_accessed=4 * total * width,
            transcendentals=length * total * width // HEAD,
        ),
        name="self_attention",
    )(scalars, queries, *cached, *new_a, *new_b)


def project_kernel(tokens_ref, weights_ref, queries_ref, keys_ref, values_ref):
    tokens = tokens_ref[...]
    queries_ref[...] = (dot(tokens, weights_ref[0]) * HEAD**-0.5).astype(jnp.bfloat16)
    keys_ref[...] = dot(tokens, weights_ref[1]).astype(jnp.bfloat16)
    values_ref[...] = dot(tokens, weights_ref[2]).astype(jnp.bfloat16)


def project(tokens, weights):
    length, depth = tokens.shape
    width = weights.shape[2]
    out = jax.ShapeDtypeStruct((length, width), jnp.bfloat16)
    return pl.pallas_call(
        project_kernel,
        out_shape=(out, out, out),
        grid=(width // 256,),
        in_specs=[
            pl.BlockSpec((length, depth), lambda c: (0, 0)),
            pl.BlockSpec((3, depth, 256), lambda c: (0, 0, c)),
        ],
        out_specs=[pl.BlockSpec((length, 256), lambda c: (0, c))] * 3,
        compiler_params=pltpu.CompilerParams(vmem_limit_bytes=VMEM_LIMIT),
        cost_estimate=pl.CostEstimate(
            flops=6 * length * depth * width, bytes_accessed=6 * depth * width, transcendentals=0
        ),
        name="project",
    )(tokens, weights)


def cross_kernel(
    core_ref,
    tokens_ref,
    context_own,
    context_far,
    output_own,
    query_own,
    cross_own,
    rows_here,
    rows_there,
    query_here,
    query_there,
    keys_own,
    values_own,
    keys_far,
    values_far,
    gains_ref,
    second_ref,
    output_far,
    query_far,
    cross_far,
    found,
    sems,
):
    core = core_ref[0]
    other = 1 - core
    half = rows_here.shape[0] // 2
    deep = query_here.shape[0]
    copies = [
        pltpu.make_async_copy(rows_here.at[pl.ds(0, half)], output_far.at[pl.ds(core * half, half)], sems.at[0]),
        pltpu.make_async_copy(rows_there.at[pl.ds(0, half)], output_far.at[pl.ds(other * half, half)], sems.at[1]),
        pltpu.make_async_copy(query_here, query_far.at[pl.ds(core * deep, deep)], sems.at[2]),
        pltpu.make_async_copy(query_there, query_far.at[pl.ds(other * deep, deep)], sems.at[3]),
        pltpu.make_async_copy(rows_here.at[pl.ds(half, half)], cross_far.at[pl.ds(core * half, half)], sems.at[4]),
        pltpu.make_async_copy(rows_there.at[pl.ds(half, half)], cross_far.at[pl.ds(other * half, half)], sems.at[5]),
    ]
    for copy in copies:
        copy.start()
    total = dot(context_own[...], output_own[...])
    copies[0].wait()
    copies[1].wait()
    total += dot(context_far[...], output_far[...])
    first = layer_norm(tokens_ref[...].astype(jnp.float32) + total, gains_ref[0:1, :]).astype(jnp.bfloat16)
    length = first.shape[0]
    lane = lax.broadcasted_iota(jnp.int32, (length, LANES), 1)
    for copy in copies[2:]:
        copy.wait()
    total = jnp.zeros((length, second_ref.shape[1]), jnp.float32)
    for query, keys, values, output in (
        (query_own, keys_own, values_own, cross_own),
        (query_far, keys_far, values_far, cross_far),
    ):
        queries = (dot(first, query[...]) * HEAD**-0.5).astype(jnp.bfloat16)
        for tile in range(keys.shape[1] // LANES):
            cut = slice(tile * LANES, (tile + 1) * LANES)
            contexts = []
            for head in range(LANES // HEAD):
                mine = (lane >= head * HEAD) & (lane < (head + 1) * HEAD)
                own = jnp.where(mine, queries[:, cut], jnp.zeros((length, LANES), jnp.bfloat16))
                scores = dot_t(own, keys[:, cut])
                raised = jnp.exp(scores - jnp.max(scores, axis=-1, keepdims=True))
                scale = 1.0 / jnp.sum(raised, axis=-1, keepdims=True)
                contexts.append(dot((raised * scale).astype(jnp.bfloat16), values[:, cut]))
            found[:, cut] = jnp.where(lane < HEAD, contexts[0], contexts[1]).astype(jnp.bfloat16)
        total += dot(found[...], output[...])
    second_ref[...] = layer_norm(first.astype(jnp.float32) + total, gains_ref[1:2, :]).astype(jnp.bfloat16)


def cross_block(core, tokens, context_own, context_far, weights, far, encoder_own, encoder_far, gains):
    length, depth = tokens.shape
    width = context_own.shape[1]
    return pl.pallas_call(
        cross_kernel,
        out_shape=jax.ShapeDtypeStruct((length, depth), jnp.bfloat16),
        in_specs=[SMEM] + [VMEM] * 6 + [ANY] * 4 + [VMEM] * 5,
        out_specs=VMEM,
        scratch_shapes=[
            pltpu.VMEM((width, depth), jnp.bfloat16),
            pltpu.VMEM((depth, width), jnp.bfloat16),
            pltpu.VMEM((width, depth), jnp.bfloat16),
            pltpu.VMEM((length, width), jnp.bfloat16),
            pltpu.SemaphoreType.DMA((6,)),
        ],
        compiler_params=pltpu.CompilerParams(vmem_limit_bytes=VMEM_LIMIT),
        cost_estimate=pl.CostEstimate(
            flops=10 * length * depth * depth, bytes_accessed=16 * width * depth, transcendentals=length * depth * 8
        ),
        name="cross_block",
    )(core, tokens, context_own, context_far, *weights, *far, *encoder_own, *encoder_far, gains)


def feed_kernel(rows_ref, expand_ref, reduce_ref, out_ref, total):
    step = pl.program_id(0)
    wide = dot(rows_ref[...], expand_ref[...])
    expanded = (0.5 * wide * (1.0 + lax.erf(wide * (0.5**0.5)))).astype(jnp.bfloat16)
    part = dot(expanded, reduce_ref[...])

    @pl.when(step == 0)
    def _():
        total[...] = part

    @pl.when(step > 0)
    def _():
        total[...] += part

    @pl.when(step == pl.num_programs(0) - 1)
    def _():
        out_ref[...] = total[...].astype(out_ref.dtype)


def feed(rows, expand_weight, reduce_weight, dtype):
    length, depth = rows.shape
    hidden = expand_weight.shape[1]
    step = 512
    return pl.pallas_call(
        feed_kernel,
        out_shape=jax.ShapeDtypeStruct((length, depth), dtype),
        grid=(hidden // step,),
        in_specs=[
            pl.BlockSpec((length, depth), lambda c: (0, 0)),
            pl.BlockSpec((depth, step), lambda c: (0, c)),
            pl.BlockSpec((step, depth), lambda c: (c, 0)),
        ],
        out_specs=pl.BlockSpec((length, depth), lambda c: (0, 0)),
        scratch_shapes=[pltpu.VMEM((length, depth), jnp.float32)],
        compiler_params=pltpu.CompilerParams(vmem_limit_bytes=VMEM_LIMIT),
        cost_estimate=pl.CostEstimate(
            flops=4 * length * depth * hidden, bytes_accessed=4 * depth * hidden, transcendentals=length * hidden
        ),
        name="feed_own" if dtype == jnp.float32 else "feed_far",
    )(rows, expand_weight, reduce_weight)


def close_kernel(scalars, second_ref, own_ref, far_ref, gains_ref, out_ref):
    live_span, row_off = scalars[1], scalars[2]
    values = second_ref[...].astype(jnp.float32) + (own_ref[...] + far_ref[...].astype(jnp.float32))
    normed = layer_norm(values, gains_ref[2:3, :])
    row = row_off + lax.broadcasted_iota(jnp.int32, normed.shape, 0)
    out_ref[...] = jnp.where(row < live_span, normed, 0.0).astype(jnp.bfloat16)


def close_rows(scalars, second, own, far, gains):
    return pl.pallas_call(
        close_kernel,
        out_shape=jax.ShapeDtypeStruct(second.shape, jnp.bfloat16),
        in_specs=[SMEM] + [VMEM] * 4,
        out_specs=VMEM,
        compiler_params=pltpu.CompilerParams(vmem_limit_bytes=VMEM_LIMIT),
        name="close_rows",
    )(scalars, second, own, far, gains)


def per_device(
    tokens,
    self_project,
    self_output,
    cross_query,
    cross_output,
    expand_weight,
    reduce_weight,
    norm_gains,
    cache_pairs,
    encoder_pairs,
    request_order,
    page_table,
    cached_length,
    span_length,
):
    devices_req = lax.axis_size("req")
    own_device = lax.axis_index("req")
    part = lax.axis_index("tensor")
    core = lax.rem(own_device, 2)
    request = request_order[own_device]
    own_count = tokens.shape[0]
    cache_rows, _, width = cache_pairs.shape
    pages_dev = cache_rows // PAGE

    pair = [(0, 1), (1, 0)]
    cores = [(r, r ^ 1) for r in range(devices_req)]
    across = [(2 * r + t, 2 * (r ^ 2) + (1 - t)) for r in range(devices_req) for t in range(2)]

    def swap(value):
        return lax.ppermute(value, "tensor", pair)

    own_targets = page_table[request]
    every_target = page_table[request_order]
    flat_cache = flat_pairs(cache_pairs)
    flat_encoder = flat_pairs(encoder_pairs)
    page_rows = flat_cache.shape[0] // pages_dev

    far_tokens = swap(tokens)
    far_encoder = swap(flat_encoder)
    half = self_output.shape[0] // 2
    deep = cross_query.shape[0] // 2
    rows_piece = jnp.concatenate(
        [
            lax.dynamic_slice_in_dim(self_output, core * half, half, 0),
            lax.dynamic_slice_in_dim(cross_output, core * half, half, 0),
        ],
        axis=0,
    )
    query_piece = lax.dynamic_slice_in_dim(cross_query, core * deep, deep, 0)
    rows_here = lax.ppermute(rows_piece, ("req", "tensor"), across)
    query_here = lax.ppermute(query_piece, ("req", "tensor"), across)
    rows_there = lax.ppermute(rows_here, "req", cores)
    query_there = lax.ppermute(query_here, "req", cores)

    outgoing = pages_call(
        own_targets // pages_dev, flat_cache.reshape(pages_dev, page_rows, LANES), devices_req, pages_dev, True
    )

    cached = split_pairs(flat_cache, width)
    own_off = part * own_count
    far_off = own_count - own_off
    live_cache, live_span = cached_length[request], span_length[request]
    own_scalars = jnp.stack([live_cache, live_span, own_off, own_off, far_off])
    far_scalars = jnp.stack([live_cache, live_span, far_off, own_off, far_off])
    own_queries, *own_new = project(tokens, self_project)
    far_queries, *far_new = project(far_tokens, self_project)
    sent_context = self_attention(far_scalars, far_queries, cached, own_new, far_new)
    far_context = swap(sent_context)
    encoder_own = split_pairs(flat_encoder, width)
    encoder_far = split_pairs(far_encoder, width)

    outgoing, _ = lax.optimization_barrier((outgoing, sent_context))
    incoming = lax.all_to_all(outgoing, "req", split_axis=0, concat_axis=0, tiled=True)

    own_context = self_attention(own_scalars, own_queries, cached, own_new, far_new)
    second = cross_block(
        core[None],
        tokens,
        own_context,
        far_context,
        (self_output, cross_query, cross_output),
        (rows_here, rows_there, query_here, query_there),
        encoder_own,
        encoder_far,
        norm_gains,
    )
    far_second = swap(second)
    own_part = feed(second, expand_weight, reduce_weight, jnp.float32)
    sent_part = feed(far_second, expand_weight, reduce_weight, jnp.bfloat16)
    far_part = swap(sent_part)
    mixed = close_rows(own_scalars[:3], second, own_part, far_part, norm_gains)

    slots = jnp.arange(pages_dev, dtype=jnp.int32)
    landing = every_target[None] == (own_device * pages_dev + slots)[:, None, None]
    sources = jnp.arange(devices_req, dtype=jnp.int32)[None, :, None]
    came_from = jnp.sum(jnp.where(landing, sources, 0), axis=(1, 2))
    pool = pages_call(came_from, incoming, pages_dev, pages_dev, False)
    return mixed, unflat_pairs(pool.reshape(-1, LANES), cache_rows, width)


def solution(mesh):
    return jax.shard_map(
        per_device,
        mesh=mesh,
        in_specs=(
            P(("req", "tensor"), None),
            P(None, None, "tensor"),
            P("tensor", None),
            P(None, "tensor"),
            P("tensor", None),
            P(None, "tensor"),
            P("tensor", None),
            P(),
            P("req", None, "tensor"),
            P("req", None, "tensor"),
            P(),
            P(),
            P(),
            P(),
        ),
        out_specs=(P(("req", "tensor"), None), P("req", None, "tensor")),
        check_vma=False,
    )
```

```python
import functools

import jax
import jax.numpy as jnp
from jax import lax
from jax.experimental import pallas as pl
from jax.experimental.pallas import tpu as pltpu
from jax.sharding import PartitionSpec as P


HEAD = 64
PAGE = 64
LANES = 128
norm_eps = 1e-05
masked_score = -1e30
MIB = 1024 * 1024
CHUNKS = 2


ANY = pl.BlockSpec(memory_space=pl.ANY)
SMEM = pl.BlockSpec(memory_space=pltpu.SMEM)
VMEM = pl.BlockSpec(memory_space=pltpu.VMEM)


def layer_norm(values, gain):
    center = values - jnp.mean(values, axis=-1, keepdims=True)
    spread = jnp.mean(center * center, axis=-1, keepdims=True)
    return center * lax.rsqrt(spread + norm_eps) * gain


def dot(a, b):
    return jnp.dot(a, b, preferred_element_type=jnp.float32)


def dot_t(a, b):
    return lax.dot_general(a, b, (((1,), (1,)), ((), ())), preferred_element_type=jnp.float32)


def pack_kernel(order_ref, table_ref, source, target, held, in_sem, out_sem):
    request = order_ref[lax.axis_index("req")]
    move_pages(lambda j: lax.div(table_ref[request, j], held.shape[0]), source, target, held, in_sem, out_sem, True)


def unpack_kernel(index_ref, source, target, held, in_sem, out_sem):
    move_pages(lambda j: index_ref[j], source, target, held, in_sem, out_sem, False)


def move_pages(index, source, target, held, in_sem, out_sem, scatter):
    count = held.shape[0]

    def load(j):
        return pltpu.make_async_copy(source.at[j if scatter else index(j)], held.at[j], in_sem.at[j])

    def store(j):
        return pltpu.make_async_copy(held.at[j], target.at[index(j) if scatter else j], out_sem.at[j])

    for j in range(count):
        load(j).start()
    for j in range(count):
        load(j).wait()
        store(j).start()
    for j in range(count):
        store(j).wait()


def pages_call(scalars, source, slots, count, scatter):
    rows = source.shape[1]
    return pl.pallas_call(
        pack_kernel if scatter else unpack_kernel,
        out_shape=jax.ShapeDtypeStruct((slots, rows, LANES), jnp.bfloat16),
        in_specs=[SMEM] * len(scalars) + [ANY],
        out_specs=ANY,
        scratch_shapes=[
            pltpu.VMEM((count, rows, LANES), jnp.bfloat16),
            pltpu.SemaphoreType.DMA((count,)),
            pltpu.SemaphoreType.DMA((count,)),
        ],
        compiler_params=pltpu.CompilerParams(vmem_limit_bytes=60 * MIB),
        cost_estimate=pl.CostEstimate(flops=0, bytes_accessed=4 * count * rows * LANES, transcendentals=0),
        name="pack_pages" if scatter else "unpack_pages",
    )(*scalars, source)


def split_kernel(pairs_ref, keys_ref, values_ref):
    groups = keys_ref.shape[1] // LANES * 2
    per = 256 // groups
    row = lax.broadcasted_iota(jnp.int32, (256, 256), 0)
    col = lax.broadcasted_iota(jnp.int32, (256, 256), 1)
    pick = (col == lax.rem(row, per) * groups + lax.div(row, per)).astype(jnp.bfloat16)
    for block in range(0, keys_ref.shape[0] // per, 2):
        both = [pairs_ref[(block + k) * 256 : (block + k + 1) * 256, :] for k in range(2)]
        got = dot(pick, jnp.concatenate(both, axis=1)).astype(jnp.bfloat16)
        for k in range(2):
            for tile in range(groups // 2):
                where = (pl.ds((block + k) * per, per), pl.ds(tile * LANES, LANES))
                lanes = slice(k * LANES, (k + 1) * LANES)
                keys_ref[where] = got[2 * tile * per : (2 * tile + 1) * per, lanes]
                values_ref[where] = got[(2 * tile + 1) * per : (2 * tile + 2) * per, lanes]


def split_pairs(pairs, width):
    rows = pairs.shape[0] * LANES // (2 * width)
    step = 512
    out = jax.ShapeDtypeStruct((rows, width), jnp.bfloat16)
    return pl.pallas_call(
        split_kernel,
        out_shape=(out, out),
        grid=(rows // step,),
        in_specs=[pl.BlockSpec((step * 2 * width // LANES, LANES), lambda i: (i, 0))],
        out_specs=[pl.BlockSpec((step, width), lambda i: (i, 0))] * 2,
        compiler_params=pltpu.CompilerParams(vmem_limit_bytes=60 * MIB),
        cost_estimate=pl.CostEstimate(
            flops=rows * 2 * width * 512, bytes_accessed=8 * rows * width, transcendentals=0
        ),
        name="split_pairs",
    )(pairs)


def flat_pairs(pairs):
    rows, _, width = pairs.shape
    return pairs.reshape(rows, 2, width // LANES, LANES).transpose(0, 2, 1, 3).reshape(-1, LANES)


def unflat_pairs(flat, rows, width):
    return flat.reshape(rows, width // LANES, 2, LANES).transpose(0, 2, 1, 3).reshape(rows, 2, width)


def self_kernel(
    order_ref, cached_ref, span_ref, queries_ref, cached_keys, cached_values, keys_a, values_a, keys_b, values_b, out_ref, *, far
):
    request = order_ref[lax.axis_index("req")]
    live_cache, live_span = cached_ref[request], span_ref[request]
    length = queries_ref.shape[0]
    new = keys_a.shape[0]
    a_off = lax.axis_index("tensor") * new
    b_off = new - a_off
    row_off = b_off if far else a_off
    slot = lax.broadcasted_iota(jnp.int32, (1, cached_keys.shape[0]), 1)
    cache_live = slot < live_cache
    row = row_off + lax.broadcasted_iota(jnp.int32, (length, new), 0)
    column = lax.broadcasted_iota(jnp.int32, (length, new), 1)
    seen = [((column + off) <= row) & ((column + off) < live_span) for off in (a_off, b_off)]
    lane = lax.broadcasted_iota(jnp.int32, (length, LANES), 1)
    queries = queries_ref[...]
    contexts = []
    for half in range(LANES // HEAD):
        mine = (lane >= half * HEAD) & (lane < (half + 1) * HEAD)
        own = jnp.where(mine, queries, jnp.zeros_like(queries))
        parts = [
            jnp.where(cache_live, dot_t(own, cached_keys[...]), masked_score),
            jnp.where(seen[0], dot_t(own, keys_a[...]), masked_score),
            jnp.where(seen[1], dot_t(own, keys_b[...]), masked_score),
        ]
        highest = functools.reduce(
            jnp.maximum, [jnp.max(part, axis=-1, keepdims=True) for part in parts]
        )
        raised = [jnp.exp(part - highest) for part in parts]
        total = sum(jnp.sum(part, axis=-1, keepdims=True) for part in raised)
        scale = 1.0 / total
        context = jnp.zeros((length, LANES), jnp.float32)
        for part, values in zip(raised, (cached_values, values_a, values_b)):
            context += dot((part * scale).astype(jnp.bfloat16), values[...])
        contexts.append(context)
    out_ref[...] = jnp.where(lane < HEAD, contexts[0], contexts[1]).astype(jnp.bfloat16)


def self_attention(lengths, queries, cached, new_a, new_b, far):
    length, width = queries.shape
    cache_rows = cached[0].shape[0]
    new = new_a[0].shape[0]

    def spec(rows):
        return pl.BlockSpec((rows, LANES), lambda c: (0, c))

    total = cache_rows + 2 * new
    return pl.pallas_call(
        functools.partial(self_kernel, far=far),
        out_shape=jax.ShapeDtypeStruct((length, width), jnp.bfloat16),
        grid=(width // LANES,),
        in_specs=[SMEM, SMEM, SMEM, spec(length), spec(cache_rows), spec(cache_rows)] + [spec(new)] * 4,
        out_specs=spec(length),
        compiler_params=pltpu.CompilerParams(vmem_limit_bytes=60 * MIB),
        cost_estimate=pl.CostEstimate(
            flops=4 * length * total * width * 4,
            bytes_accessed=4 * total * width,
            transcendentals=length * total * width // HEAD,
        ),
        name="self_far" if far else "self_own",
    )(*lengths, queries, *cached, *new_a, *new_b)


def project_kernel(tokens_ref, weights_ref, queries_ref, keys_ref, values_ref):
    tokens = tokens_ref[...]
    queries_ref[...] = (dot(tokens, weights_ref[0]) * HEAD**-0.5).astype(jnp.bfloat16)
    keys_ref[...] = dot(tokens, weights_ref[1]).astype(jnp.bfloat16)
    values_ref[...] = dot(tokens, weights_ref[2]).astype(jnp.bfloat16)


def project(tokens, weights):
    length, depth = tokens.shape
    width = weights.shape[2]
    out = jax.ShapeDtypeStruct((length, width), jnp.bfloat16)
    return pl.pallas_call(
        project_kernel,
        out_shape=(out, out, out),
        grid=(width // 256,),
        in_specs=[
            pl.BlockSpec((length, depth), lambda c: (0, 0)),
            pl.BlockSpec((3, depth, 256), lambda c: (0, 0, c)),
        ],
        out_specs=[pl.BlockSpec((length, 256), lambda c: (0, c))] * 3,
        compiler_params=pltpu.CompilerParams(vmem_limit_bytes=60 * MIB),
        cost_estimate=pl.CostEstimate(
            flops=6 * length * depth * width, bytes_accessed=6 * depth * width, transcendentals=0
        ),
        name="project",
    )(tokens, weights)


def cross_kernel(
    tokens_ref,
    context_own,
    context_far,
    output_own,
    query_own,
    cross_own,
    rows_here,
    rows_there,
    query_here,
    query_there,
    keys_own,
    values_own,
    keys_far,
    values_far,
    gains_ref,
    second_ref,
    output_far,
    query_far,
    cross_far,
    found,
    sems,
):
    core = lax.rem(lax.axis_index("req"), 2)
    other = 1 - core
    half = rows_here.shape[0] // 2
    deep = query_here.shape[0]
    copies = [
        pltpu.make_async_copy(rows_here.at[pl.ds(0, half)], output_far.at[pl.ds(core * half, half)], sems.at[0]),
        pltpu.make_async_copy(rows_there.at[pl.ds(0, half)], output_far.at[pl.ds(other * half, half)], sems.at[1]),
        pltpu.make_async_copy(query_here, query_far.at[pl.ds(core * deep, deep)], sems.at[2]),
        pltpu.make_async_copy(query_there, query_far.at[pl.ds(other * deep, deep)], sems.at[3]),
        pltpu.make_async_copy(rows_here.at[pl.ds(half, half)], cross_far.at[pl.ds(core * half, half)], sems.at[4]),
        pltpu.make_async_copy(rows_there.at[pl.ds(half, half)], cross_far.at[pl.ds(other * half, half)], sems.at[5]),
    ]
    for copy in copies:
        copy.start()
    total = dot(context_own[...], output_own[...])
    copies[0].wait()
    copies[1].wait()
    total += dot(context_far[...], output_far[...])
    first = layer_norm(tokens_ref[...].astype(jnp.float32) + total, gains_ref[0:1, :]).astype(jnp.bfloat16)
    length = first.shape[0]
    lane = lax.broadcasted_iota(jnp.int32, (length, LANES), 1)
    for copy in copies[2:]:
        copy.wait()
    total = jnp.zeros((length, second_ref.shape[1]), jnp.float32)
    for query, keys, values, output in (
        (query_own, keys_own, values_own, cross_own),
        (query_far, keys_far, values_far, cross_far),
    ):
        queries = (dot(first, query[...]) * HEAD**-0.5).astype(jnp.bfloat16)
        for tile in range(keys.shape[1] // LANES):
            cut = slice(tile * LANES, (tile + 1) * LANES)
            contexts = []
            for head in range(LANES // HEAD):
                mine = (lane >= head * HEAD) & (lane < (head + 1) * HEAD)
                own = jnp.where(mine, queries[:, cut], jnp.zeros((length, LANES), jnp.bfloat16))
                scores = dot_t(own, keys[:, cut])
                raised = jnp.exp(scores - jnp.max(scores, axis=-1, keepdims=True))
                scale = 1.0 / jnp.sum(raised, axis=-1, keepdims=True)
                contexts.append(dot((raised * scale).astype(jnp.bfloat16), values[:, cut]))
            found[:, cut] = jnp.where(lane < HEAD, contexts[0], contexts[1]).astype(jnp.bfloat16)
        total += dot(found[...], output[...])
    second_ref[...] = layer_norm(first.astype(jnp.float32) + total, gains_ref[1:2, :]).astype(jnp.bfloat16)


def cross_block(tokens, context_own, context_far, weights, far, encoder_own, encoder_far, gains):
    length, depth = tokens.shape
    width = context_own.shape[1]
    return pl.pallas_call(
        cross_kernel,
        out_shape=jax.ShapeDtypeStruct((length, depth), jnp.bfloat16),
        in_specs=[VMEM] * 6 + [ANY] * 4 + [VMEM] * 5,
        out_specs=VMEM,
        scratch_shapes=[
            pltpu.VMEM((width, depth), jnp.bfloat16),
            pltpu.VMEM((depth, width), jnp.bfloat16),
            pltpu.VMEM((width, depth), jnp.bfloat16),
            pltpu.VMEM((length, width), jnp.bfloat16),
            pltpu.SemaphoreType.DMA((6,)),
        ],
        compiler_params=pltpu.CompilerParams(vmem_limit_bytes=60 * MIB),
        cost_estimate=pl.CostEstimate(
            flops=10 * length * depth * depth, bytes_accessed=16 * width * depth, transcendentals=length * depth * 8
        ),
        name="cross_block",
    )(tokens, context_own, context_far, *weights, *far, *encoder_own, *encoder_far, gains)


def feed_kernel(rows_ref, expand_ref, reduce_ref, out_ref, total):
    step = pl.program_id(0)
    wide = dot(rows_ref[...], expand_ref[...])
    expanded = (0.5 * wide * (1.0 + lax.erf(wide * (0.5**0.5)))).astype(jnp.bfloat16)
    part = dot(expanded, reduce_ref[...])

    @pl.when(step == 0)
    def _():
        total[...] = part

    @pl.when(step > 0)
    def _():
        total[...] += part

    @pl.when(step == pl.num_programs(0) - 1)
    def _():
        out_ref[...] = total[...].astype(out_ref.dtype)


def feed(rows, expand_weight, reduce_weight, dtype):
    length, depth = rows.shape
    hidden = expand_weight.shape[1]
    step = 512
    return pl.pallas_call(
        feed_kernel,
        out_shape=jax.ShapeDtypeStruct((length, depth), dtype),
        grid=(hidden // step,),
        in_specs=[
            pl.BlockSpec((length, depth), lambda c: (0, 0)),
            pl.BlockSpec((depth, step), lambda c: (0, c)),
            pl.BlockSpec((step, depth), lambda c: (c, 0)),
        ],
        out_specs=pl.BlockSpec((length, depth), lambda c: (0, 0)),
        scratch_shapes=[pltpu.VMEM((length, depth), jnp.float32)],
        compiler_params=pltpu.CompilerParams(vmem_limit_bytes=24 * MIB),
        cost_estimate=pl.CostEstimate(
            flops=4 * length * depth * hidden, bytes_accessed=4 * depth * hidden, transcendentals=length * hidden
        ),
        name="feed_own" if dtype == jnp.float32 else "feed_far",
    )(rows, expand_weight, reduce_weight)


def close_kernel(order_ref, span_ref, second_ref, own_ref, gains_ref, *rest):
    *far_refs, out_ref = rest
    live_span = span_ref[order_ref[lax.axis_index("req")]]
    row_off = lax.axis_index("tensor") * second_ref.shape[0]
    chunk = far_refs[0].shape[0]
    for k, far_ref in enumerate(far_refs):
        rows = pl.ds(k * chunk, chunk)
        values = second_ref[rows].astype(jnp.float32) + (own_ref[rows] + far_ref[...].astype(jnp.float32))
        normed = layer_norm(values, gains_ref[2:3, :])
        row = row_off + k * chunk + lax.broadcasted_iota(jnp.int32, normed.shape, 0)
        out_ref[rows] = jnp.where(row < live_span, normed, 0.0).astype(jnp.bfloat16)


def close_rows(lengths, second, own, far, gains):
    return pl.pallas_call(
        close_kernel,
        out_shape=jax.ShapeDtypeStruct(second.shape, jnp.bfloat16),
        in_specs=[SMEM] * 2 + [VMEM] * (3 + len(far)),
        out_specs=VMEM,
        compiler_params=pltpu.CompilerParams(vmem_limit_bytes=16 * MIB),
        name="close_rows",
    )(*lengths, second, own, gains, *far)


def per_device(
    tokens,
    self_project,
    self_output,
    cross_query,
    cross_output,
    expand_weight,
    reduce_weight,
    norm_gains,
    cache_pairs,
    encoder_pairs,
    request_order,
    page_table,
    cached_length,
    span_length,
):
    devices_req = lax.axis_size("req")
    own_device = lax.axis_index("req")
    core = lax.rem(own_device, 2)
    cache_rows, _, width = cache_pairs.shape
    pages_dev = cache_rows // PAGE

    pair = [(0, 1), (1, 0)]
    cores = [(r, r ^ 1) for r in range(devices_req)]
    across = [(2 * r + t, 2 * (r ^ 2) + (1 - t)) for r in range(devices_req) for t in range(2)]

    def swap(value):
        return lax.ppermute(value, "tensor", pair)

    flat_cache = flat_pairs(cache_pairs)
    flat_encoder = flat_pairs(encoder_pairs)
    page_rows = flat_cache.shape[0] // pages_dev

    far_tokens = swap(tokens)
    far_encoder = swap(flat_encoder)
    half = self_output.shape[0] // 2
    deep = cross_query.shape[0] // 2
    rows_piece = jnp.concatenate(
        [
            lax.dynamic_slice_in_dim(self_output, core * half, half, 0),
            lax.dynamic_slice_in_dim(cross_output, core * half, half, 0),
        ],
        axis=0,
    )
    query_piece = lax.dynamic_slice_in_dim(cross_query, core * deep, deep, 0)
    rows_here = lax.ppermute(rows_piece, ("req", "tensor"), across)
    query_here = lax.ppermute(query_piece, ("req", "tensor"), across)
    rows_there = lax.ppermute(rows_here, "req", cores)
    query_there = lax.ppermute(query_here, "req", cores)

    outgoing = pages_call(
        (request_order, page_table), flat_cache.reshape(pages_dev, page_rows, LANES), devices_req, pages_dev, True
    )

    lengths = (request_order, cached_length, span_length)
    own_queries, *own_new = project(tokens, self_project)
    cached = split_pairs(flat_cache, width)
    far_queries, *far_new = project(far_tokens, self_project)
    sent_context = self_attention(lengths, far_queries, cached, own_new, far_new, True)
    far_context = swap(sent_context)
    encoder_own = split_pairs(flat_encoder, width)
    encoder_far = split_pairs(far_encoder, width)

    outgoing, _ = lax.optimization_barrier((outgoing, sent_context))
    incoming = lax.all_to_all(outgoing, "req", split_axis=0, concat_axis=0, tiled=True)

    own_context = self_attention(lengths, own_queries, cached, own_new, far_new, False)
    second = cross_block(
        tokens,
        own_context,
        far_context,
        (self_output, cross_query, cross_output),
        (rows_here, rows_there, query_here, query_there),
        encoder_own,
        encoder_far,
        norm_gains,
    )
    chunk = second.shape[0] // CHUNKS
    far_second = [swap(second[k * chunk : (k + 1) * chunk]) for k in range(CHUNKS)]
    own_part = feed(second, expand_weight, reduce_weight, jnp.float32)
    far_part = []
    for k in range(CHUNKS):
        sent_part = feed(far_second[k], expand_weight, reduce_weight, jnp.bfloat16)
        far_part.append(swap(sent_part))
    mixed = close_rows((request_order, span_length), second, own_part, far_part, norm_gains)

    slots = jnp.arange(pages_dev, dtype=jnp.int32)
    landing = page_table[None] == (own_device * pages_dev + slots)[:, None, None]
    sources = jnp.sum(
        jnp.where(
            jnp.arange(devices_req, dtype=jnp.int32)[:, None] == request_order[None, :],
            jnp.arange(request_order.shape[0], dtype=jnp.int32)[None, :],
            0,
        ),
        axis=1,
    )
    came_from = jnp.sum(jnp.where(landing, sources[None, :, None], 0), axis=(1, 2))
    pool = pages_call((came_from,), incoming, pages_dev, pages_dev, False)
    return mixed, unflat_pairs(pool.reshape(-1, LANES), cache_rows, width)


def solution(mesh):
    return jax.shard_map(
        per_device,
        mesh=mesh,
        in_specs=(
            P(("req", "tensor"), None),
            P(None, None, "tensor"),
            P("tensor", None),
            P(None, "tensor"),
            P("tensor", None),
            P(None, "tensor"),
            P("tensor", None),
            P(),
            P("req", None, "tensor"),
            P("req", None, "tensor"),
            P(),
            P(),
            P(),
            P(),
        ),
        out_specs=(P(("req", "tensor"), None), P("req", None, "tensor")),
        check_vma=False,
    )
```
